32 devices in a mesh: row: 4 (over x, core), col: 8 (over z, y).
Axes of the slice: x: 2, y: 2, z: 4, core: 2. Of those that a mesh axis runs over, the one named last changes fastest.
Arguments:
- x_vals: bfloat16 [256, 32, 4096], P(('row', 'col')), may hold values from -6 to 6
- occupancy: int32 [256, 32], P(('row', 'col')), may hold values from 0 to 1, as said below
- perm: int32 [256], replicated, may hold values from 0 to 255, as said below
Outputs:
- sign_iterate_next: bfloat16 [16384, 16384], P('row', 'col')
The draws below stay inside these ranges and needn't reach their ends.
Inputs may be any that keep to these rules, and one draw needn't show every extreme that they name: occupancy[i, s] = 1 marks block (i, (i - 16 + s) mod 256) as present; the diagonal slot s = 16 is always 1, and some row has all 32 slots 1. perm is a permutation with perm[j] = a(j mod (8)) * 32 + b(j div (8)) for permutations a and b; so the 32 band columns of any row fall exactly 4 times into each aligned run of 32 new indices, and each aligned run of 64 initial indices has exactly 16 members in each aligned run of 64 new indices.
All inputs are finite; a program needn't handle non-finite values.
Results may differ from the reference program's by a relative error of at most 0.0017.
Values may be sent and summed in bfloat16 or wider, within the bound.
A program may use at most 128 MiB of HBM per device.

```python
import jax
import jax.numpy as jnp
from jax import lax

BLOCK_EDGE = 64
NB = 256
W = 32
CP = 32


def draw_occupancy(key, part):
    key_keep = jax.random.fold_in(key, 11)
    key_full = jax.random.fold_in(key, 12)
    key_pick = jax.random.fold_in(key, 13)
    kept_slots = jax.random.randint(key_keep, (NB, W), 0, 5) < 3
    full_rows = jax.random.randint(key_full, (NB,), 0, 8) == 0
    forced = jnp.arange(NB) == jax.random.randint(key_pick, (), 0, NB)
    diagonal = (jnp.arange(W) == W // 2)[None, :]
    present_mask = kept_slots | diagonal | (full_rows | forced)[:, None]
    return present_mask.astype(jnp.int32)


def draw_perm(key, part):
    residues = NB // CP
    column_map = jax.random.permutation(jax.random.fold_in(key, 21), residues)
    within_map = jax.random.permutation(jax.random.fold_in(key, 22), CP)
    index_all = jnp.arange(NB)
    return (column_map[index_all % residues] * CP + within_map[index_all // residues]).astype(jnp.int32)


def block_scale(own_key, shape, cuts, smallest, top_value):
    def one(dim, parts):
        heights = jax.random.uniform(jax.random.fold_in(jax.random.fold_in(own_key, 6), dim), (parts,), jnp.float32, smallest / len(cuts), top_value / len(cuts))
        return jnp.repeat(jnp.exp(heights), shape[dim] // parts).reshape((-1,) + (1,) * (len(shape) - dim - 1))

    factor_of = one(*cuts[0])
    for cut in cuts[1:]:
        factor_of = factor_of * one(*cut)
    return factor_of


def scatter_about(rng, dims, width, limit, shards=(), kind=jnp.bfloat16):
    array = jax.random.normal(rng, dims, jnp.float32) * width
    if len(shards) > 0:
        array = block_scale(rng, dims, shards, -0.22, 0.18) * array
    return jnp.clip(array, min=-limit, max=limit).astype(kind)


def setup_inputs(seed: int = 0) -> dict:
    seeds = jax.random.split(jax.random.key(seed), 4)
    return {
        "x_vals": scatter_about(seeds[0], (NB, W, BLOCK_EDGE * BLOCK_EDGE), 1.0, 6.0, ((0, 32),)),
        "occupancy": draw_occupancy(jax.random.fold_in(seeds[3], 71), 0),
        "perm": draw_perm(jax.random.fold_in(seeds[3], 71), 0),
    }


def filtered_rows(left_vals, right_vals, block_cols):
    band_extent = block_cols.shape[1]
    slot_ids = jnp.arange(band_extent, dtype=jnp.int32)

    def one_row(inputs):
        row_vals, row_cols = inputs
        present_mask = row_cols >= 0
        source = jnp.where(present_mask, row_cols, 0).astype(jnp.int32)
        found_cols = block_cols[source]
        matched = (found_cols[:, None, :] == row_cols[None, :, None]) & present_mask[:, None, None] & present_mask[None, :, None]
        located = jnp.any(matched, axis=2)
        which_slot = jnp.sum(matched.astype(jnp.int32) * slot_ids[None, None, :], axis=2).astype(jnp.int32)
        chosen = right_vals[source[:, None], which_slot]
        chosen = jnp.where(located[:, :, None], chosen, jnp.zeros_like(chosen))
        left_factor_blocks = row_vals.reshape(band_extent, BLOCK_EDGE, BLOCK_EDGE).astype(jnp.float32)
        right_factor_blocks = chosen.reshape(band_extent, band_extent, BLOCK_EDGE, BLOCK_EDGE).astype(jnp.float32)
        return jnp.einsum("exp,egpk->gxk", left_factor_blocks, right_factor_blocks).reshape(band_extent, BLOCK_EDGE * BLOCK_EDGE)

    return lax.map(one_row, (left_vals, block_cols))


def reference(x_vals, occupancy, perm):
    index_all = jnp.arange(NB, dtype=jnp.int32)
    inverse = jnp.zeros((NB,), jnp.int32).at[perm].set(index_all)
    orig_cols = (index_all[:, None] - W // 2 + jnp.arange(W, dtype=jnp.int32)[None, :]) % NB
    present_mask = occupancy == 1
    new_cols = jnp.where(present_mask, perm[orig_cols], -1).astype(jnp.int32)
    kept_vals = jnp.where(present_mask[:, :, None], x_vals, jnp.zeros_like(x_vals))
    relaid = kept_vals[inverse]
    relaid_cols = new_cols[inverse]
    square = filtered_rows(relaid, relaid, relaid_cols).astype(jnp.bfloat16)
    cube_vals = filtered_rows(relaid, square, relaid_cols)
    stepped_matrix = (1.5 * relaid.astype(jnp.float32) - (0.5 / (BLOCK_EDGE * W)) * cube_vals).astype(jnp.bfloat16)
    alive_slot = relaid_cols >= 0
    stepped_matrix = jnp.where(alive_slot[:, :, None], stepped_matrix, jnp.zeros_like(stepped_matrix))
    target = jnp.where(alive_slot, relaid_cols, 0).astype(jnp.int32)
    blocks = jnp.zeros((NB, NB, BLOCK_EDGE * BLOCK_EDGE), jnp.bfloat16).at[index_all[:, None], target].add(stepped_matrix)
    return blocks.reshape(NB, NB, BLOCK_EDGE, BLOCK_EDGE).transpose(0, 2, 1, 3).reshape(NB * BLOCK_EDGE, NB * BLOCK_EDGE)
```

```python
import jax
import jax.numpy as jnp
from jax import lax
from jax.experimental import pallas as pl
from jax.experimental.pallas import tpu as pltpu
from jax.sharding import PartitionSpec as P

BLOCK_EDGE = 64


def multiply_kernel(order_ref, left_ref, far0, far1, far2, far3, out_ref):
    width = out_ref.shape[-1]
    left = left_ref[...].reshape(-1, width)
    right = jnp.concatenate([r[...].reshape(-1, width) for r in (far0, far1, far2, far3)], axis=0)
    update = jnp.dot(left, right, preferred_element_type=jnp.float32).reshape(out_ref.shape)

    @pl.when(pl.program_id(1) == 0)
    def _():
        out_ref[...] = update

    @pl.when(pl.program_id(1) != 0)
    def _():
        out_ref[...] += update


def banded_product(left, far, order, residue_major, slots):
    panels, halves, count, edge, width = left.shape
    chunk = slots // 2
    chunks = count // chunk

    def far_spec(position):
        def chunk_of(g):
            return lax.rem(2 * g + chunks - 1 + lax.rem(position + 1 + 2 * g, 4), chunks)

        if residue_major:
            return pl.BlockSpec(
                (1, chunk, edge, width), lambda g, p, order: (order[p], chunk_of(g), 0, 0)
            )
        return pl.BlockSpec(
            (chunk, 1, edge, width), lambda g, p, order: (chunk_of(g), order[p], 0, 0)
        )

    return pl.pallas_call(
        multiply_kernel,
        out_shape=jax.ShapeDtypeStruct((halves, count, edge, width), jnp.float32),
        grid_spec=pltpu.PrefetchScalarGridSpec(
            num_scalar_prefetch=1,
            grid=(count // slots, panels),
            in_specs=[
                pl.BlockSpec(
                    (1, halves, slots, edge, width), lambda g, p, order: (p, 0, g, 0, 0)
                )
            ]
            + [far_spec(position) for position in range(4)],
            out_specs=pl.BlockSpec((halves, slots, edge, width), lambda g, p, order: (0, g, 0, 0)),
        ),
        compiler_params=pltpu.CompilerParams(dimension_semantics=("arbitrary", "arbitrary")),
    )(order, left, far, far, far, far)


def spread_kernel(source_ref, target_ref, rows_ref, out_ref):
    slots = rows_ref.shape[-1] // BLOCK_EDGE
    q, n = pl.program_id(0), pl.program_id(1)
    row = q * pl.num_programs(1) + source_ref[n]
    out_ref[...] = jnp.zeros_like(out_ref)
    for v in range(slots):
        block = rows_ref[0, 0, :, v * BLOCK_EDGE : (v + 1) * BLOCK_EDGE].astype(jnp.float32)
        target = target_ref[row * slots + v]
        odd = lax.rem(target, 2)
        pair = jnp.concatenate(
            [block * (1 - odd).astype(jnp.float32), block * odd.astype(jnp.float32)], axis=1
        ).astype(out_ref.dtype)
        at = pl.multiple_of((target // 2) * (2 * BLOCK_EDGE), 2 * BLOCK_EDGE)
        out_ref[:, pl.ds(at, 2 * BLOCK_EDGE)] += pair


def spread(rows, source, target, panel_cols):
    halves, count, edge, width = rows.shape
    return pl.pallas_call(
        spread_kernel,
        out_shape=jax.ShapeDtypeStruct((halves * count * edge, panel_cols * edge), rows.dtype),
        grid_spec=pltpu.PrefetchScalarGridSpec(
            num_scalar_prefetch=2,
            grid=(halves, count),
            in_specs=[
                pl.BlockSpec((1, 1, edge, width), lambda q, n, source, target: (q, source[n], 0, 0))
            ],
            out_specs=pl.BlockSpec(
                (edge, panel_cols * edge), lambda q, n, source, target: (q * count + n, 0)
            ),
        ),
        compiler_params=pltpu.CompilerParams(dimension_semantics=("arbitrary", "arbitrary")),
    )(source, target, rows)


def band_index(m, row_residue, col_residue, slots):
    first = m - slots // 2 + (col_residue < row_residue).astype(jnp.int32)
    v = jnp.arange(slots, dtype=jnp.int32)
    first = first[..., None]
    return first + (v - first) % slots


def widen(values, index, slots):
    high = (index % (2 * slots)) >= slots
    high = jnp.repeat(high, BLOCK_EDGE, axis=-1)[..., None, :]
    zero = jnp.zeros((), values.dtype)
    return jnp.concatenate(
        [jnp.where(high, zero, values), jnp.where(high, values, zero)], axis=-1
    )


def shards(x_vals, occupancy, perm):
    row_devices = lax.axis_size("row")
    panels = lax.axis_size("col")
    own_row = lax.axis_index("row")
    own_col = lax.axis_index("col")
    local_rows, band_extent, block_area = x_vals.shape
    block_count = perm.shape[0]
    panel_cols = block_count // panels
    halves = panels // row_devices
    slots = band_extent // panels
    lanes = slots * BLOCK_EDGE

    panel_of_residue = perm[:panels] // panel_cols
    residue_ids = jnp.arange(panels, dtype=jnp.int32)
    order = jnp.sum(
        jnp.where(panel_of_residue[None, :] == residue_ids[:, None], residue_ids[None, :], 0), axis=1
    ).astype(jnp.int32)
    inside = perm[::panels] % panel_cols
    m_ids = jnp.arange(panel_cols, dtype=jnp.int32)
    source = jnp.sum(
        jnp.where(inside[None, :] == m_ids[:, None], m_ids[None, :], 0), axis=1
    ).astype(jnp.int32)
    own_residue = order[own_col]
    row_residues = lax.dynamic_slice_in_dim(order, own_row * halves, halves)

    first_row = (own_row * panels + own_col) * local_rows
    row_ids = first_row + jnp.arange(local_rows, dtype=jnp.int32)
    cols = (
        row_ids[:, None] - band_extent // 2 + jnp.arange(band_extent, dtype=jnp.int32)[None, :]
    ) % block_count
    placed = (
        (occupancy[:, :, None, None] == 1)
        & ((cols % panels)[:, :, None, None] == order[None, None, :, None])
        & (
            ((cols // panels) % slots)[:, :, None, None]
            == jnp.arange(slots, dtype=jnp.int32)[None, None, None, :]
        )
    ).astype(jnp.bfloat16)
    kept = jnp.sum(placed.astype(jnp.float32), axis=1).astype(jnp.bfloat16)
    every_kept = lax.all_gather(
        kept.reshape(local_rows, panels * slots), ("row", "col"), axis=0, tiled=True
    ).reshape(panel_cols, panels, panels, slots)
    values = jnp.einsum(
        "kspt,ksf->pktf", placed, x_vals, preferred_element_type=jnp.float32
    ).astype(jnp.bfloat16)
    values = (
        values.reshape(panels, local_rows, slots, BLOCK_EDGE, BLOCK_EDGE)
        .transpose(0, 1, 3, 2, 4)
        .reshape(panels, local_rows, BLOCK_EDGE, lanes)
    )
    first = lax.all_to_all(values, "col", split_axis=0, concat_axis=0, tiled=True)
    first = first.reshape(panels * local_rows, BLOCK_EDGE, lanes)
    far = lax.all_gather(first, "row", axis=0, tiled=True).reshape(
        panel_cols, panels, BLOCK_EDGE, lanes
    )
    tile = jnp.stack(
        [
            lax.dynamic_index_in_dim(far, row_residues[q], axis=1, keepdims=False)
            for q in range(halves)
        ]
    )
    own_kept = lax.dynamic_index_in_dim(every_kept, own_col, axis=2, keepdims=False)
    wanted = jnp.stack(
        [
            lax.dynamic_index_in_dim(own_kept, row_residues[q], axis=1, keepdims=False)
            for q in range(halves)
        ]
    )
    wanted = wanted > 0
    left = lax.all_gather(tile[None], "col", axis=0, tiled=True)

    far_index = band_index(m_ids[:, None], residue_ids[None, :], own_residue, slots)
    far_wide = widen(far, far_index, slots)
    left_index = band_index(
        m_ids[None, None, :], row_residues[None, :, None], order[:, None, None], slots
    )
    left_wide = widen(left, left_index, slots)
    tile_index = band_index(m_ids[None, :], row_residues[:, None], own_residue, slots)
    tile_high = (tile_index % (2 * slots)) >= slots

    def spread_mask(mask):
        return jnp.repeat(mask, BLOCK_EDGE, axis=-1)[:, :, None, :]

    def narrow(wide):
        chosen = jnp.where(spread_mask(tile_high), wide[..., lanes:], wide[..., :lanes])
        return jnp.where(spread_mask(wanted), chosen, 0.0)

    square = narrow(banded_product(left_wide, far_wide, order, False, slots)).astype(jnp.bfloat16)
    far_square = lax.all_gather(square, "row", axis=0, tiled=True)
    square_index = band_index(m_ids[None, :], order[:, None], own_residue, slots)
    square_wide = widen(far_square, square_index, slots)
    cube = narrow(banded_product(left_wide, square_wide, residue_ids, True, slots))
    stepped = (
        1.5 * tile.astype(jnp.float32) - 0.5 / (BLOCK_EDGE * band_extent) * cube
    ).astype(jnp.bfloat16)
    hit = (tile_index % panel_cols)[..., None] == m_ids
    target = jnp.sum(jnp.where(hit, inside, 0), axis=-1).astype(jnp.int32).reshape(-1)
    return spread(stepped, source, target, panel_cols)


def solution(mesh):
    return jax.shard_map(
        shards,
        mesh=mesh,
        in_specs=(P(("row", "col"), None, None), P(("row", "col"), None), P()),
        out_specs=P("row", "col"),
        check_vma=False,
    )
```
